512 devices in a mesh: pipe: 8 (over y_lo, x), dp: 64 (over z, y_hi, core).
Axes of the slice: x: 4, y: 4 (y_hi: 2, y_lo: 2; y = y_hi * 2 + y_lo), z: 16, core: 2. Of those that a mesh axis runs over, the one named last changes fastest.
Arguments:
- visual_fragments: bfloat16 [8, 64, 64, 1152], P(None, 'dp'), may hold values from -6 to 6
- widening_kernel: bfloat16 [8, 1152, 2176], P('pipe', None, 'dp'), may hold values from -0.1875 to 0.1875
- narrowing_kernel: bfloat16 [8, 2176, 1152], P('pipe', 'dp'), may hold values from -0.125 to 0.125
- caption_outputs: bfloat16 [4608, 1152], P(('pipe', 'dp')), may hold values from -6 to 6
- earlier_averaged: float32 [4096, 1152], P(('pipe', 'dp')), may hold values from -6 to 6
- match_targets: int32 [4608], replicated, may hold values from 0 to 4607, each once
- score_scaling: float32 [1], replicated, may hold values from 5 to 15
- score_shift: float32 [1], replicated, may hold values from -4 to -2
Outputs:
- image_grad: float32 [4608, 1152], P(('pipe', 'dp'))
- text_grad: float32 [4608, 1152], P(('pipe', 'dp'))
The draws below stay inside these ranges and needn't reach their ends.
Inputs may be any that keep to these rules, and one draw needn't show every extreme that they name: match_targets is a permutation: every text is the positive of exactly one image.
All inputs are finite; a program needn't handle non-finite values.
Results may differ from the reference program's by a relative error of at most 0.017.
Values may be sent and summed in bfloat16 or wider, within the bound.
No kernel may reach another device: no remote copies, remote signals or barrier semaphores. Data moves between devices by JAX's collectives and lax.ppermute only.
A program may use at most 128 MiB of HBM per device.

```python
import math
import jax
import jax.numpy as jnp
from jax import lax

E = 1152
FFW = 2176
PATCH = 64
IMG_MB = 1
PRIOR_DEV = 8
LAYERS = 8
MICRO = 8
IMG_MICRO = 64
TOWER_IMAGES = 512
PRIOR = 4096
IMAGES = 4608
TEXTS = 4608
N_PIPE = 8
N_DP = 64


def shard_levels(stream_key, dims, cuts, least, high):
    loudness, own = 1.0, jax.random.fold_in(stream_key, 6)
    for position, shards_of in cuts:
        draws = jnp.exp(jax.random.uniform(jax.random.fold_in(own, position), (shards_of,), jnp.float32, least / len(cuts), high / len(cuts)))
        loudness = loudness * jnp.repeat(draws, dims[position] // shards_of).reshape([-1 if axis == position else 1 for axis in range(len(dims))])
    return loudness


def centred(rng, shape, scale, reach, split=(), kind=jnp.bfloat16):
    entries = jax.random.normal(rng, shape, jnp.float32) * scale
    if len(split) > 0:
        entries = shard_levels(rng, shape, split, -0.22, 0.18) * entries
    return jnp.clip(entries, min=-reach, max=reach).astype(kind)


def setup_inputs(seed: int = 0) -> dict:
    key_of = jax.random.split(jax.random.key(seed), 9)
    visual_fragments = centred(key_of[0], (MICRO, IMG_MICRO, PATCH, E), 1.0, 6.0, ((1, 64),))
    widening_kernel = centred(key_of[1], (LAYERS, E, FFW), E ** -0.5, 0.1875, ((0, 8), (2, 64)))
    narrowing_kernel = centred(key_of[2], (LAYERS, FFW, E), FFW ** -0.5, 0.125, ((0, 8), (1, 64)))
    caption_outputs = centred(key_of[3], (TEXTS, E), 1.0, 6.0, ((0, 512),))
    earlier_averaged = centred(key_of[4], (PRIOR, E), 1.0, 6.0, ((0, 512),), jnp.float32)
    match_targets = jax.random.permutation(key_of[5], IMAGES).astype(jnp.int32)
    score_scaling = jnp.clip(jnp.exp(jax.random.uniform(key_of[6], (1,), jnp.float32, math.log(5.0), math.log(15.0))), 5.0, 15.0)
    score_shift = jnp.clip(jax.random.uniform(key_of[7], (1,), jnp.float32, -4.0, -2.0), -4.0, -2.0)
    return dict(visual_fragments=visual_fragments, widening_kernel=widening_kernel, narrowing_kernel=narrowing_kernel, caption_outputs=caption_outputs, earlier_averaged=earlier_averaged, match_targets=match_targets, score_scaling=score_scaling, score_shift=score_shift)


def layer_norm(hidden_rows):
    values = hidden_rows.astype(jnp.float32)
    centre = lax.optimization_barrier(jnp.mean(values, axis=-1, keepdims=True))
    shifted = values - centre
    variance = lax.optimization_barrier(jnp.mean(shifted * shifted, axis=-1, keepdims=True))
    return (shifted * lax.rsqrt(variance + 1e-06)).astype(jnp.bfloat16)

def section_block(hidden_rows, w_up, w_down):
    normed = layer_norm(hidden_rows)
    pre_act = jnp.dot(normed, w_up, preferred_element_type=jnp.float32)
    activated = jax.nn.gelu(pre_act, approximate=True).astype(jnp.bfloat16)
    updated = hidden_rows.astype(jnp.float32) + jnp.dot(activated, w_down, preferred_element_type=jnp.float32)
    return updated.astype(jnp.bfloat16)

def unit_rows(values):
    values = values.astype(jnp.float32)
    total = lax.optimization_barrier(jnp.sum(values * values, axis=-1, keepdims=True))
    return (values * lax.rsqrt(total + 1e-06)).astype(jnp.bfloat16)

def coupling_factors(picture_group, source_caption_tile, match_entries, target_tile, sharpness_factor, shift_addend):
    similarity_scores = sharpness_factor * jnp.dot(picture_group, source_caption_tile.T, preferred_element_type=jnp.float32) + shift_addend
    matching_couples = match_entries[:, None] == target_tile[None, :]
    coefficient_grid = jnp.where(matching_couples, -sharpness_factor * jax.nn.sigmoid(-similarity_scores), sharpness_factor * jax.nn.sigmoid(similarity_scores))
    return coefficient_grid.astype(jnp.bfloat16)

def reference(visual_fragments, widening_kernel, narrowing_kernel, caption_outputs, earlier_averaged, match_targets, score_scaling, score_shift):

    def one_micro(micro_tokens):
        tokens = micro_tokens.reshape(IMG_MICRO * PATCH, E)
        for layer in range(LAYERS):
            tokens = section_block(tokens, widening_kernel[layer], narrowing_kernel[layer])
        return lax.optimization_barrier(jnp.mean(tokens.astype(jnp.float32).reshape(IMG_MICRO, PATCH, E), axis=1))
    pooled = lax.map(one_micro, visual_fragments).reshape(TOWER_IMAGES, E)
    tower_emb = unit_rows(pooled).reshape(N_PIPE * N_DP, IMG_MB, E)
    prior_emb = unit_rows(earlier_averaged).reshape(N_PIPE * N_DP, PRIOR_DEV, E)
    picture_vectors = jnp.concatenate([tower_emb, prior_emb], axis=1).reshape(IMAGES, E)
    caption_vectors = unit_rows(caption_outputs)
    target_tile = jnp.arange(TEXTS, dtype=jnp.int32)
    coefficient_grid = coupling_factors(picture_vectors, caption_vectors, match_targets, target_tile, score_scaling[0], score_shift[0])
    image_grad = jnp.dot(coefficient_grid, caption_vectors, preferred_element_type=jnp.float32)
    text_grad = jnp.dot(coefficient_grid.T, picture_vectors, preferred_element_type=jnp.float32)
    return (image_grad, text_grad)
```

```python
import functools

import jax
import jax.numpy as jnp
from jax import lax
from jax.experimental import pallas as pl
from jax.experimental.pallas import tpu as pltpu
from jax.sharding import Mesh, PartitionSpec as P

STAGE_GAP = 2
GROUP = 1
PLANE = ("pipe", "yh", "core")
EVERY = ("pipe", "z", "yh", "core")


def unit_rows(values):
    values = values.astype(jnp.float32)
    total = jnp.sum(values * values, axis=-1, keepdims=True)
    return (values * lax.rsqrt(total + 1e-06)).astype(jnp.bfloat16)


def share_rows(rows, axes, count):
    copies = jnp.broadcast_to(rows[None], (count,) + rows.shape)
    return lax.all_to_all(copies, axes, 0, 0)


def swap(value, axis):
    return lax.ppermute(value, axis, [(0, 1), (1, 0)])


def stage_kernel(first_ref, panel_ref, carried_ref, up_a, down_a, up_b, down_b, out_ref, pooled_ref, normed_ref, hidden_ref, act_ref, *, take, wide, narrow):
    rows, width = carried_ref.shape
    if take == "panel":
        hidden = panel_ref[0].astype(jnp.float32)
    elif take == "carried":
        hidden = carried_ref[...].astype(jnp.float32)
    else:
        fresh = panel_ref[0].astype(jnp.float32)
        moved = carried_ref[...].astype(jnp.float32)
        hidden = jnp.where(first_ref[0] == 1, fresh, moved)
    centre = jnp.mean(hidden, axis=-1, keepdims=True)
    shifted = hidden - centre
    variance = jnp.mean(shifted * shifted, axis=-1, keepdims=True)
    normed = (shifted * lax.rsqrt(variance + 1e-06)).astype(jnp.bfloat16)
    normed_ref[...] = normed
    units = up_a.shape[0]
    for half, up_ref in enumerate((up_a, up_b)):

        @pl.loop(0, units // wide)
        def _(index, half=half, up_ref=up_ref):
            at = pl.multiple_of(index * wide, wide)
            pre_act = lax.dot_general(
                normed_ref[...],
                up_ref[pl.ds(at, wide), :],
                (((1,), (1,)), ((), ())),
                preferred_element_type=jnp.float32,
            )
            to = pl.multiple_of(half * units + index * wide, 128)
            act_ref[:, pl.ds(to, wide)] = jax.nn.gelu(pre_act, approximate=True).astype(jnp.bfloat16)

    hidden_ref[...] = hidden.astype(jnp.bfloat16)

    @pl.loop(0, width // narrow)
    def _(index):
        at = pl.multiple_of(index * narrow, narrow)
        total = hidden_ref[:, pl.ds(at, narrow)].astype(jnp.float32)
        total += jnp.dot(act_ref[:, :units], down_a[:, pl.ds(at, narrow)], preferred_element_type=jnp.float32)
        total += jnp.dot(act_ref[:, units:], down_b[:, pl.ds(at, narrow)], preferred_element_type=jnp.float32)
        updated = total.astype(jnp.bfloat16)
        out_ref[:, pl.ds(at, narrow)] = updated
        images = pooled_ref.shape[0]
        for image in range(images):
            patches = rows // images
            mean = jnp.mean(updated[image * patches : (image + 1) * patches].astype(jnp.float32), axis=0, keepdims=True)
            pooled_ref[image : image + 1, pl.ds(at, narrow)] = mean


def stage(first, panels, pick, carried, weights, images, take, wide=384, narrow=384):
    rows, width = carried.shape
    units = weights[0].shape[0]
    whole = pl.BlockSpec(memory_space=pltpu.VMEM)
    return pl.pallas_call(
        functools.partial(stage_kernel, take=take, wide=wide, narrow=narrow),
        grid_spec=pltpu.PrefetchScalarGridSpec(
            num_scalar_prefetch=1,
            grid=(1,),
            in_specs=[
                pl.BlockSpec((1, rows, width), lambda i, first: (pick, 0, 0)),
                pl.BlockSpec((rows, width), lambda i, first: (0, 0)),
                whole,
                whole,
                whole,
                whole,
            ],
            out_specs=[
                pl.BlockSpec((rows, width), lambda i, first: (0, 0)),
                pl.BlockSpec((images, width), lambda i, first: (0, 0)),
            ],
            scratch_shapes=[
                pltpu.VMEM((rows, width), jnp.bfloat16),
                pltpu.VMEM((rows, width), jnp.bfloat16),
                pltpu.VMEM((rows, 2 * units), jnp.bfloat16),
            ],
        ),
        out_shape=[
            jax.ShapeDtypeStruct((rows, width), jnp.bfloat16),
            jax.ShapeDtypeStruct((images, width), jnp.float32),
        ],
        compiler_params=pltpu.CompilerParams(vmem_limit_bytes=24 << 20),
        cost_estimate=pl.CostEstimate(
            flops=8 * rows * width * units,
            bytes_accessed=8 * width * units,
            transcendentals=2 * rows * units,
        ),
        name="stage",
    )(first, panels, carried, *weights)


def pair_weights(images, texts, targets, columns, scale, shift):
    scores = scale * lax.dot_general(
        images, texts, (((1,), (1,)), ((), ())), preferred_element_type=jnp.float32
    ) + shift
    grid = jnp.where(
        targets[:, None] == columns[None, :],
        -scale * jax.nn.sigmoid(-scores),
        scale * jax.nn.sigmoid(scores),
    )
    return grid.astype(jnp.bfloat16)


def across(grid, other):
    return lax.dot_general(grid, other, (((0,), (0,)), ((), ())), preferred_element_type=jnp.float32)


def body(
    visual_fragments,
    widening_kernel,
    narrowing_kernel,
    caption_outputs,
    earlier_averaged,
    match_targets,
    score_scaling,
    score_shift,
):
    stages = lax.axis_size("pipe")
    depth = lax.axis_size("z")
    stage_id = lax.axis_index("pipe")
    z_id = lax.axis_index("z")
    around = lax.axis_size("yh") * lax.axis_size("core")
    around_id = lax.axis_index("yh") * lax.axis_size("core") + lax.axis_index("core")
    micros, img_mb, patch_count, width = visual_fragments.shape
    tok_rows = img_mb * patch_count
    plane = stages * around
    scale = score_scaling[0]
    shift = score_shift[0]
    texts_dev = caption_outputs.shape[0]
    prior_dev = earlier_averaged.shape[0]

    up = widening_kernel[0].T
    down = narrowing_kernel[0]
    both = jnp.stack([up, down])
    both = jnp.concatenate([both, swap(both, "yh")], axis=1)
    units = both.shape[1]
    padded = -(-units // 8) * 8
    both = jnp.pad(both, ((0, 0), (0, padded - units), (0, 0)))
    up_own = lax.all_gather(both[0], "z", axis=0, tiled=True)
    down_own = lax.all_gather(both[1], "z", axis=0, tiled=True)

    text_own = unit_rows(caption_outputs)
    prior_own = unit_rows(earlier_averaged)
    texts = share_rows(text_own, "z", depth).reshape(depth * texts_dev, width)
    priors = share_rows(prior_own, PLANE, plane).reshape(plane * prior_dev, width)
    labels = lax.dynamic_index_in_dim(
        match_targets.reshape(stages, depth, around, img_mb + prior_dev), z_id, 1, keepdims=False
    )
    columns = (
        ((stage_id * depth + jnp.arange(depth, dtype=jnp.int32)) * around + around_id) * texts_dev
    )[:, None] + jnp.arange(texts_dev, dtype=jnp.int32)[None, :]
    columns = columns.reshape(-1)
    grid = pair_weights(priors, texts, labels[:, :, img_mb:].reshape(-1), columns, scale, shift)
    prior_part = jnp.dot(grid, texts, preferred_element_type=jnp.float32).astype(jnp.bfloat16)
    prior_part = lax.all_to_all(prior_part.reshape(plane, prior_dev, width), PLANE, 0, 0)
    prior_grad = jnp.sum(prior_part.astype(jnp.float32), axis=0)
    text_early = across(grid, priors)
    up_own, down_own, prior_grad, text_early = lax.optimization_barrier((up_own, down_own, prior_grad, text_early))
    weights = (up_own, down_own, swap(up_own, "core"), swap(down_own, "core"))

    groups = micros // GROUP
    panels = visual_fragments.reshape(groups, GROUP * tok_rows, width)
    first = (stage_id == 0).astype(jnp.int32).reshape(1)
    ring = [(source, (source + 1) % stages) for source in range(stages)]
    last = STAGE_GAP * (stages - 1)
    sent = []
    pooled = []
    for slot in range(groups + last):
        pick = min(slot, groups - 1)
        if slot < STAGE_GAP:
            take, carried = "panel", panels[pick]
        else:
            take, carried = ("either" if slot < groups else "carried"), sent[slot - STAGE_GAP]
        moved, mean = stage(first, panels, pick, carried, weights, GROUP * img_mb, take)
        if slot >= last:
            pooled.append(mean)
        sent.append(lax.ppermute(moved, "pipe", ring) if slot < last + groups - STAGE_GAP else None)
    tower_own = unit_rows(jnp.concatenate(pooled, axis=0))

    tower = share_rows(tower_own, PLANE, plane).reshape(stages, around, micros, width)[stages - 1]
    tower = tower.reshape(around * micros, width)
    tower_labels = labels[:, :, 0].T.reshape(-1)
    tower_grid = pair_weights(tower, texts, tower_labels, columns, scale, shift)
    tower_part = jnp.dot(tower_grid, texts, preferred_element_type=jnp.float32).astype(jnp.bfloat16)
    tower_part = tower_part.reshape(around, micros, width).transpose(1, 0, 2).reshape(plane, img_mb, width)
    tower_part = lax.all_to_all(tower_part, PLANE, 0, 0)
    tower_grad = jnp.sum(tower_part.astype(jnp.float32), axis=0)
    text_part = text_early + across(tower_grid, tower)
    text_part = text_part.astype(jnp.bfloat16).reshape(depth, texts_dev, width)
    text_grad = jnp.sum(lax.all_to_all(text_part, "z", 0, 0).astype(jnp.float32), axis=0)
    return jnp.concatenate([tower_grad, prior_grad], axis=0), text_grad


def solution(mesh):
    sizes = dict(mesh.shape)
    stages = sizes["pipe"]
    fine = Mesh(mesh.devices.reshape(stages, sizes["dp"] // 4, 2, 2), EVERY)
    data = ("z", "yh", "core")
    placed = (
        P(None, data, None, None),
        P("pipe", None, data),
        P("pipe", data, None),
        P(EVERY, None),
        P(EVERY, None),
        P(),
        P(),
        P(),
    )
    return jax.shard_map(
        body,
        mesh=fine,
        in_specs=placed,
        out_specs=(P(EVERY, None), P(EVERY, None)),
        check_vma=False,
    )
```

```python
import functools

import jax
import jax.numpy as jnp
from jax import lax
from jax.experimental import pallas as pl
from jax.experimental.pallas import tpu as pltpu
from jax.sharding import Mesh, PartitionSpec as P

STAGE_GAP = 2
GROUP = 1
PLANE = ("pipe", "yh", "core")
EVERY = ("pipe", "z", "yh", "core")


def unit_rows(values):
    values = values.astype(jnp.float32)
    total = jnp.sum(values * values, axis=-1, keepdims=True)
    return (values * lax.rsqrt(total + 1e-06)).astype(jnp.bfloat16)


def share_rows(rows, axes, count):
    copies = jnp.broadcast_to(rows[None], (count,) + rows.shape)
    return lax.all_to_all(copies, axes, 0, 0)


def swap(value, axis):
    return lax.ppermute(value, axis, [(0, 1), (1, 0)])


def stage_kernel(*refs, take, pick, images, wide, narrow):
    refs = list(refs)
    if take == "either":
        first_ref = refs.pop(0)
    panels_ref = refs.pop(0) if take != "carried" else None
    carried_ref = refs.pop(0) if take != "panel" else None
    up_a, down_a, up_b, down_b, out_ref = refs[:5]
    pooled_ref = refs[5] if images else None
    normed_ref, hidden_ref, act_ref = refs[-3:]
    rows, width = out_ref.shape
    if take == "panel":
        hidden = panels_ref[pick]
    elif take == "carried":
        hidden = carried_ref[...]
    else:
        hidden = jnp.where(first_ref[0] == 1, panels_ref[pick], carried_ref[...])
    hidden_ref[...] = hidden
    values = hidden.astype(jnp.float32)
    centre = jnp.mean(values, axis=-1, keepdims=True)
    shifted = values - centre
    variance = jnp.mean(shifted * shifted, axis=-1, keepdims=True)
    normed_ref[...] = (shifted * lax.rsqrt(variance + 1e-06)).astype(jnp.bfloat16)
    units = up_a.shape[0]

    def widen(at, half, up_ref):
        pre_act = lax.dot_general(
            normed_ref[...],
            up_ref[pl.ds(at, wide), :],
            (((1,), (1,)), ((), ())),
            preferred_element_type=jnp.float32,
        )
        to = half * units + at
        act_ref[:, pl.ds(to, wide)] = jax.nn.gelu(pre_act, approximate=True).astype(jnp.bfloat16)

    def tighten(at):
        total = hidden_ref[:, pl.ds(at, narrow)].astype(jnp.float32)
        total += jnp.dot(act_ref[:, :units], down_a[:, pl.ds(at, narrow)], preferred_element_type=jnp.float32)
        total += jnp.dot(act_ref[:, units:], down_b[:, pl.ds(at, narrow)], preferred_element_type=jnp.float32)
        updated = total.astype(jnp.bfloat16)
        out_ref[:, pl.ds(at, narrow)] = updated
        for image in range(images):
            patches = rows // images
            mean = jnp.mean(updated[image * patches : (image + 1) * patches].astype(jnp.float32), axis=0, keepdims=True)
            pooled_ref[image : image + 1, pl.ds(at, narrow)] = mean

    for half, up_ref in enumerate((up_a, up_b)):
        if wide == units:
            widen(0, half, up_ref)
        else:

            @pl.loop(0, units // wide)
            def _(index, half=half, up_ref=up_ref):
                widen(pl.multiple_of(index * wide, 128), half, up_ref)

    if narrow == width:
        tighten(0)
    else:

        @pl.loop(0, width // narrow)
        def _(index):
            tighten(pl.multiple_of(index * narrow, 128))


def stage(first, panels, pick, carried, weights, images, take, wide=1152, narrow=1152):
    rows, width = panels.shape[1:]
    units = weights[0].shape[0]
    whole = pl.BlockSpec(memory_space=pltpu.VMEM)
    operands = {"panel": (panels,), "carried": (carried,), "either": (panels, carried)}[take] + tuple(weights)
    specs = [whole] * len(operands)
    if take == "either":
        operands = (first,) + operands
        specs = [pl.BlockSpec(memory_space=pltpu.SMEM)] + specs
    shapes = [jax.ShapeDtypeStruct((rows, width), jnp.bfloat16)]
    if images:
        shapes.append(jax.ShapeDtypeStruct((images, width), jnp.float32))
    return pl.pallas_call(
        functools.partial(stage_kernel, take=take, pick=pick, images=images, wide=wide, narrow=narrow),
        in_specs=specs,
        out_specs=[whole] * len(shapes),
        out_shape=shapes,
        scratch_shapes=[
            pltpu.VMEM((rows, width), jnp.bfloat16),
            pltpu.VMEM((rows, width), jnp.bfloat16),
            pltpu.VMEM((rows, 2 * units), jnp.bfloat16),
        ],
        compiler_params=pltpu.CompilerParams(vmem_limit_bytes=24 << 20),
        cost_estimate=pl.CostEstimate(
            flops=8 * rows * width * units,
            bytes_accessed=8 * width * units,
            transcendentals=2 * rows * units,
        ),
        name="stage",
    )(*operands)


def pair_weights(images, texts, targets, columns, scale, shift):
    scores = scale * lax.dot_general(
        images, texts, (((1,), (1,)), ((), ())), preferred_element_type=jnp.float32
    ) + shift
    grid = jnp.where(
        targets[:, None] == columns[None, :],
        -scale * jax.nn.sigmoid(-scores),
        scale * jax.nn.sigmoid(scores),
    )
    return grid.astype(jnp.bfloat16)


def across(grid, other):
    return lax.dot_general(grid, other, (((0,), (0,)), ((), ())), preferred_element_type=jnp.float32)


def body(
    visual_fragments,
    widening_kernel,
    narrowing_kernel,
    caption_outputs,
    earlier_averaged,
    match_targets,
    score_scaling,
    score_shift,
):
    stages = lax.axis_size("pipe")
    depth = lax.axis_size("z")
    stage_id = lax.axis_index("pipe")
    z_id = lax.axis_index("z")
    around = lax.axis_size("yh") * lax.axis_size("core")
    around_id = lax.axis_index("yh") * lax.axis_size("core") + lax.axis_index("core")
    micros, img_mb, patch_count, width = visual_fragments.shape
    tok_rows = img_mb * patch_count
    plane = stages * around
    scale = score_scaling[0]
    shift = score_shift[0]
    texts_dev = caption_outputs.shape[0]
    prior_dev = earlier_averaged.shape[0]

    up = widening_kernel[0].T
    down = narrowing_kernel[0]
    both = jnp.stack([up, down])
    both = jnp.concatenate([both, swap(both, "yh")], axis=1)
    units = both.shape[1]
    padded = -(-units // 8) * 8
    both = jnp.pad(both, ((0, 0), (0, padded - units), (0, 0)))
    depth_blocks = lax.all_gather(both.reshape(2 * padded, width), "z", axis=0, tiled=True)

    text_own = unit_rows(caption_outputs)
    prior_own = unit_rows(earlier_averaged)
    lanes = texts_dev * width // 128
    texts = share_rows(text_own.reshape(lanes, 128), "z", depth).reshape(depth * texts_dev, width)
    priors = share_rows(prior_own, PLANE, plane).reshape(plane * prior_dev, width)
    labels = lax.dynamic_index_in_dim(
        match_targets.reshape(stages, depth, around, img_mb + prior_dev), z_id, 1, keepdims=False
    )
    columns = (
        ((stage_id * depth + jnp.arange(depth, dtype=jnp.int32)) * around + around_id) * texts_dev
    )[:, None] + jnp.arange(texts_dev, dtype=jnp.int32)[None, :]
    columns = columns.reshape(-1)
    grid = pair_weights(priors, texts, labels[:, :, img_mb:].reshape(-1), columns, scale, shift)
    prior_part = jnp.dot(grid, texts, preferred_element_type=jnp.float32).astype(jnp.bfloat16)
    prior_part = lax.all_to_all(prior_part.reshape(plane, prior_dev, width), PLANE, 0, 0)
    prior_grad = jnp.sum(prior_part.astype(jnp.float32), axis=0)
    text_early = across(grid, priors)
    first = (stage_id == 0).astype(jnp.int32).reshape(1)
    depth_blocks, prior_grad, text_early, first = lax.optimization_barrier((depth_blocks, prior_grad, text_early, first))
    depth_blocks = depth_blocks.reshape(depth, 2, padded, width)
    up_own = depth_blocks[:, 0].reshape(depth * padded, width)
    down_own = depth_blocks[:, 1].reshape(depth * padded, width)
    weights = (up_own, down_own, swap(up_own, "core"), swap(down_own, "core"))

    groups = micros // GROUP
    panels = visual_fragments.reshape(groups, GROUP * tok_rows, width)
    ring = [(source, (source + 1) % stages) for source in range(stages)]
    last = STAGE_GAP * (stages - 1)
    sent = []
    pooled = []
    for slot in range(groups + last):
        pick = min(slot, groups - 1)
        if slot < STAGE_GAP:
            take, carried = "panel", panels[pick]
        else:
            take, carried = ("either" if slot < groups else "carried"), sent[slot - STAGE_GAP]
        done = slot >= last
        results = stage(first, panels, pick, carried, weights, GROUP * img_mb if done else 0, take)
        moved = results[0]
        if done:
            pooled.append(results[1])
        sent.append(lax.ppermute(moved, "pipe", ring) if slot < last + groups - STAGE_GAP else None)
    tower_own = unit_rows(jnp.concatenate(pooled, axis=0))

    tower = share_rows(tower_own, PLANE, plane).reshape(stages, around, micros, width)[stages - 1]
    tower = tower.reshape(around * micros, width)
    tower_labels = labels[:, :, 0].T.reshape(-1)
    tower_grid = pair_weights(tower, texts, tower_labels, columns, scale, shift)
    text_part = text_early + across(tower_grid, tower)
    text_part = text_part.astype(jnp.bfloat16).reshape(depth, lanes, 128)
    text_grad = jnp.sum(lax.all_to_all(text_part, "z", 0, 0).astype(jnp.float32), axis=0)
    text_grad = text_grad.reshape(texts_dev, width)
    tower_part = jnp.dot(tower_grid, texts, preferred_element_type=jnp.float32).astype(jnp.bfloat16)
    tower_part = tower_part.reshape(around, micros, width).transpose(1, 0, 2).reshape(plane, img_mb, width)
    tower_part = lax.all_to_all(tower_part, PLANE, 0, 0)
    tower_grad = jnp.sum(tower_part.astype(jnp.float32), axis=0)
    return jnp.concatenate([tower_grad, prior_grad], axis=0), text_grad


def solution(mesh):
    sizes = dict(mesh.shape)
    stages = sizes["pipe"]
    fine = Mesh(mesh.devices.reshape(stages, sizes["dp"] // 4, 2, 2), EVERY)
    data = ("z", "yh", "core")
    placed = (
        P(None, data, None, None),
        P("pipe", None, data),
        P("pipe", data, None),
        P(EVERY, None),
        P(EVERY, None),
        P(),
        P(),
        P(),
    )
    return jax.shard_map(
        body,
        mesh=fine,
        in_specs=placed,
        out_specs=(P(EVERY, None), P(EVERY, None)),
        check_vma=False,
    )
```

```python
import functools

import jax
import jax.numpy as jnp
from jax import lax
from jax.experimental import pallas as pl
from jax.experimental.pallas import tpu as pltpu
from jax.sharding import Mesh, PartitionSpec as P

STAGE_GAP = 2
GROUP = 1
PLANE = ("pipe", "yh", "core")
EVERY = ("pipe", "z", "yh", "core")


def unit_rows(values):
    values = values.astype(jnp.float32)
    total = jnp.sum(values * values, axis=-1, keepdims=True)
    return (values * lax.rsqrt(total + 1e-06)).astype(jnp.bfloat16)


def share_rows(rows, axes, count):
    copies = jnp.broadcast_to(rows[None], (count,) + rows.shape)
    return lax.all_to_all(copies, axes, 0, 0)


def swap(value, axis):
    return lax.ppermute(value, axis, [(0, 1), (1, 0)])


def stage_kernel(*refs, take, pick, images):
    refs = list(refs)
    if take == "either":
        first_ref = refs.pop(0)
    panels_ref = refs.pop(0) if take != "carried" else None
    carried_ref = refs.pop(0) if take != "panel" else None
    own_ref, other_ref, out_ref = refs[:3]
    pooled_ref = refs[3] if images else None
    (act_ref,) = refs[-1:]
    rows, width = out_ref.shape
    if take == "panel":
        hidden = panels_ref[pick]
    elif take == "carried":
        hidden = carried_ref[...]
    else:
        hidden = jnp.where(first_ref[0] == 1, panels_ref[pick], carried_ref[...])
    values = hidden.astype(jnp.float32)
    centre = jnp.mean(values, axis=-1, keepdims=True)
    shifted = values - centre
    variance = jnp.mean(shifted * shifted, axis=-1, keepdims=True)
    normed = (shifted * lax.rsqrt(variance + 1e-06)).astype(jnp.bfloat16)
    blocks, _, block, _ = own_ref.shape
    units = blocks * block
    total = values
    for half, ref in enumerate((own_ref, other_ref)):
        pre_act = lax.dot_general(
            normed,
            ref[:, 0].reshape(units, width),
            (((1,), (1,)), ((), ())),
            preferred_element_type=jnp.float32,
        )
        act_ref[:, half * units : (half + 1) * units] = jax.nn.gelu(pre_act, approximate=True).astype(jnp.bfloat16)
    for half, ref in enumerate((own_ref, other_ref)):
        total += jnp.dot(
            act_ref[:, half * units : (half + 1) * units],
            ref[:, 1].reshape(units, width),
            preferred_element_type=jnp.float32,
        )
    updated = total.astype(jnp.bfloat16)
    out_ref[...] = updated
    for image in range(images):
        patches = rows // images
        mean = jnp.mean(updated[image * patches : (image + 1) * patches].astype(jnp.float32), axis=0, keepdims=True)
        pooled_ref[image : image + 1] = mean


def stage(first, panels, pick, carried, weights, images, take):
    rows, width = panels.shape[1:]
    units = weights[0].shape[0] * weights[0].shape[2]
    whole = pl.BlockSpec(memory_space=pltpu.VMEM)
    operands = {"panel": (panels,), "carried": (carried,), "either": (panels, carried)}[take] + tuple(weights)
    specs = [whole] * len(operands)
    if take == "either":
        operands = (first,) + operands
        specs = [pl.BlockSpec(memory_space=pltpu.SMEM)] + specs
    shapes = [jax.ShapeDtypeStruct((rows, width), jnp.bfloat16)]
    if images:
        shapes.append(jax.ShapeDtypeStruct((images, width), jnp.float32))
    return pl.pallas_call(
        functools.partial(stage_kernel, take=take, pick=pick, images=images),
        in_specs=specs,
        out_specs=[whole] * len(shapes),
        out_shape=shapes,
        scratch_shapes=[
            pltpu.VMEM((rows, 2 * units), jnp.bfloat16),
        ],
        compiler_params=pltpu.CompilerParams(vmem_limit_bytes=24 << 20),
        cost_estimate=pl.CostEstimate(
            flops=8 * rows * width * units,
            bytes_accessed=8 * width * units,
            transcendentals=2 * rows * units,
        ),
        name="stage",
    )(*operands)


def pair_weights(images, texts, targets, columns, scale, shift):
    scores = scale * lax.dot_general(
        images, texts, (((1,), (1,)), ((), ())), preferred_element_type=jnp.float32
    ) + shift
    grid = jnp.where(
        targets[:, None] == columns[None, :],
        -scale * jax.nn.sigmoid(-scores),
        scale * jax.nn.sigmoid(scores),
    )
    return grid.astype(jnp.bfloat16)


def across(grid, other):
    return lax.dot_general(grid, other, (((0,), (0,)), ((), ())), preferred_element_type=jnp.float32)


def body(
    visual_fragments,
    widening_kernel,
    narrowing_kernel,
    caption_outputs,
    earlier_averaged,
    match_targets,
    score_scaling,
    score_shift,
):
    stages = lax.axis_size("pipe")
    depth = lax.axis_size("z")
    stage_id = lax.axis_index("pipe")
    z_id = lax.axis_index("z")
    around = lax.axis_size("yh") * lax.axis_size("core")
    around_id = lax.axis_index("yh") * lax.axis_size("core") + lax.axis_index("core")
    micros, img_mb, patch_count, width = visual_fragments.shape
    tok_rows = img_mb * patch_count
    plane = stages * around
    scale = score_scaling[0]
    shift = score_shift[0]
    texts_dev = caption_outputs.shape[0]
    prior_dev = earlier_averaged.shape[0]

    up = widening_kernel[0].T
    down = narrowing_kernel[0]
    both = jnp.stack([up, down])
    both = jnp.concatenate([both, swap(both, "yh")], axis=1)
    units = both.shape[1]
    padded = -(-units // 8) * 8
    both = jnp.pad(both, ((0, 0), (0, padded - units), (0, 0)))
    depth_blocks = lax.all_gather(both.reshape(2 * padded, width), "z", axis=0, tiled=True)

    text_own = unit_rows(caption_outputs)
    prior_own = unit_rows(earlier_averaged)
    lanes = texts_dev * width // 128
    texts = lax.all_gather(text_own, "z", axis=0, tiled=False).reshape(depth * texts_dev, width)
    priors = share_rows(prior_own, PLANE, plane).reshape(plane * prior_dev, width)
    labels = lax.dynamic_index_in_dim(
        match_targets.reshape(stages, depth, around, img_mb + prior_dev), z_id, 1, keepdims=False
    )
    columns = (
        ((stage_id * depth + jnp.arange(depth, dtype=jnp.int32)) * around + around_id) * texts_dev
    )[:, None] + jnp.arange(texts_dev, dtype=jnp.int32)[None, :]
    columns = columns.reshape(-1)
    grid = pair_weights(priors, texts, labels[:, :, img_mb:].reshape(-1), columns, scale, shift)
    prior_part = jnp.dot(grid, texts, preferred_element_type=jnp.float32).astype(jnp.bfloat16)
    prior_part = lax.all_to_all(prior_part.reshape(plane, prior_dev, width), PLANE, 0, 0)
    prior_grad = jnp.sum(prior_part.astype(jnp.float32), axis=0)
    text_early = across(grid, priors)
    first = (stage_id == 0).astype(jnp.int32).reshape(1)
    depth_blocks, prior_grad, text_early, first = lax.optimization_barrier((depth_blocks, prior_grad, text_early, first))
    other_blocks = swap(depth_blocks, "core")
    weights = tuple(half.reshape(depth, 2, padded, width) for half in (depth_blocks, other_blocks))

    groups = micros // GROUP
    panels = visual_fragments.reshape(groups, GROUP * tok_rows, width)
    ring = [(source, (source + 1) % stages) for source in range(stages)]
    last = STAGE_GAP * (stages - 1)
    sent = []
    pooled = []
    for slot in range(groups + last):
        pick = min(slot, groups - 1)
        if slot < STAGE_GAP:
            take, carried = "panel", panels[pick]
        else:
            take, carried = ("either" if slot < groups else "carried"), sent[slot - STAGE_GAP]
        done = slot >= last
        results = stage(first, panels, pick, carried, weights, GROUP * img_mb if done else 0, take)
        moved = results[0]
        if done:
            pooled.append(results[1])
        sent.append(lax.ppermute(moved, "pipe", ring) if slot < last + groups - STAGE_GAP else None)
    tower_own = unit_rows(jnp.concatenate(pooled, axis=0))

    tower = share_rows(tower_own, PLANE, plane).reshape(stages, around, micros, width)[stages - 1]
    tower = tower.reshape(around * micros, width)
    tower_labels = labels[:, :, 0].T.reshape(-1)
    tower_grid = pair_weights(tower, texts, tower_labels, columns, scale, shift)
    text_part = text_early + across(tower_grid, tower)
    text_part = text_part.astype(jnp.bfloat16).reshape(depth, lanes, 128)
    text_part = lax.all_to_all(text_part, "z", 0, 0)
    tower_part = jnp.dot(tower_grid, texts, preferred_element_type=jnp.float32).astype(jnp.bfloat16)
    tower_part = tower_part.reshape(around, micros, width).transpose(1, 0, 2)
    tower_part = tower_part.reshape(plane, img_mb * width // 128, 128)
    text_part, tower_part = lax.optimization_barrier((text_part, tower_part))
    text_grad = jnp.sum(text_part.astype(jnp.float32), axis=0).reshape(texts_dev, width)
    tower_part = lax.all_to_all(tower_part, PLANE, 0, 0)
    tower_grad = jnp.sum(tower_part.astype(jnp.float32), axis=0).reshape(img_mb, width)
    return jnp.concatenate([tower_grad, prior_grad], axis=0), text_grad


def solution(mesh):
    sizes = dict(mesh.shape)
    stages = sizes["pipe"]
    fine = Mesh(mesh.devices.reshape(stages, sizes["dp"] // 4, 2, 2), EVERY)
    data = ("z", "yh", "core")
    placed = (
        P(None, data, None, None),
        P("pipe", None, data),
        P("pipe", data, None),
        P(EVERY, None),
        P(EVERY, None),
        P(),
        P(),
        P(),
    )
    return jax.shard_map(
        body,
        mesh=fine,
        in_specs=placed,
        out_specs=(P(EVERY, None), P(EVERY, None)),
        check_vma=False,
    )
```

```python
import functools

import jax
import jax.numpy as jnp
from jax import lax
from jax.experimental import pallas as pl
from jax.experimental.pallas import tpu as pltpu
from jax.sharding import Mesh, PartitionSpec as P

STAGE_GAP = 2
GROUP = 1
PLANE = ("pipe", "yh", "core")
EVERY = ("pipe", "z", "yh", "core")


def unit_rows(values):
    values = values.astype(jnp.float32)
    total = jnp.sum(values * values, axis=-1, keepdims=True)
    return (values * lax.rsqrt(total + 1e-06)).astype(jnp.bfloat16)


def share_rows(rows, axes, count):
    copies = jnp.broadcast_to(rows[None], (count,) + rows.shape)
    return lax.all_to_all(copies, axes, 0, 0)


def swap(value, axis):
    return lax.ppermute(value, axis, [(0, 1), (1, 0)])


def stage_kernel(*refs, take, pick, images):
    refs = list(refs)
    if take == "either":
        first_ref = refs.pop(0)
    panels_ref = refs.pop(0) if take != "carried" else None
    carried_ref = refs.pop(0) if take != "panel" else None
    own_ref, other_ref, out_ref = refs[:3]
    pooled_ref = refs[3] if images else None
    (act_ref,) = refs[-1:]
    rows, width = out_ref.shape
    if take == "panel":
        hidden = panels_ref[pick]
    elif take == "carried":
        hidden = carried_ref[...]
    else:
        hidden = jnp.where(first_ref[0] == 1, panels_ref[pick], carried_ref[...])
    values = hidden.astype(jnp.float32)
    centre = jnp.mean(values, axis=-1, keepdims=True)
    shifted = values - centre
    variance = jnp.mean(shifted * shifted, axis=-1, keepdims=True)
    normed = (shifted * lax.rsqrt(variance + 1e-06)).astype(jnp.bfloat16)
    blocks, _, block, _ = own_ref.shape
    units = blocks * block
    total = values
    for half, ref in enumerate((own_ref, other_ref)):
        pre_act = lax.dot_general(
            normed,
            ref[:, 0].reshape(units, width),
            (((1,), (1,)), ((), ())),
            preferred_element_type=jnp.float32,
        )
        act_ref[:, half * units : (half + 1) * units] = jax.nn.gelu(pre_act, approximate=True).astype(jnp.bfloat16)
    for half, ref in enumerate((own_ref, other_ref)):
        total += jnp.dot(
            act_ref[:, half * units : (half + 1) * units],
            ref[:, 1].reshape(units, width),
            preferred_element_type=jnp.float32,
        )
    updated = total.astype(jnp.bfloat16)
    out_ref[...] = updated
    for image in range(images):
        patches = rows // images
        mean = jnp.mean(updated[image * patches : (image + 1) * patches].astype(jnp.float32), axis=0, keepdims=True)
        pooled_ref[image : image + 1] = mean


def stage(first, panels, pick, carried, weights, images, take):
    rows, width = panels.shape[1:]
    units = weights[0].shape[0] * weights[0].shape[2]
    whole = pl.BlockSpec(memory_space=pltpu.VMEM)
    operands = {"panel": (panels,), "carried": (carried,), "either": (panels, carried)}[take] + tuple(weights)
    specs = [whole] * len(operands)
    if take == "either":
        operands = (first,) + operands
        specs = [pl.BlockSpec(memory_space=pltpu.SMEM)] + specs
    shapes = [jax.ShapeDtypeStruct((rows, width), jnp.bfloat16)]
    if images:
        shapes.append(jax.ShapeDtypeStruct((images, width), jnp.float32))
    return pl.pallas_call(
        functools.partial(stage_kernel, take=take, pick=pick, images=images),
        in_specs=specs,
        out_specs=[whole] * len(shapes),
        out_shape=shapes,
        scratch_shapes=[
            pltpu.VMEM((rows, 2 * units), jnp.bfloat16),
        ],
        compiler_params=pltpu.CompilerParams(vmem_limit_bytes=24 << 20),
        cost_estimate=pl.CostEstimate(
            flops=8 * rows * width * units,
            bytes_accessed=8 * width * units,
            transcendentals=2 * rows * units,
        ),
        name="stage",
    )(*operands)


def place_kernel(blocks_ref, placed_ref, sem):
    copy = pltpu.make_async_copy(blocks_ref, placed_ref, sem)
    copy.start()
    copy.wait()


def place(blocks):
    return pl.pallas_call(
        place_kernel,
        in_specs=[pl.BlockSpec(memory_space=pltpu.VMEM)],
        out_specs=pl.BlockSpec(memory_space=pltpu.VMEM),
        out_shape=jax.ShapeDtypeStruct(blocks.shape, blocks.dtype),
        scratch_shapes=[pltpu.SemaphoreType.DMA],
        compiler_params=pltpu.CompilerParams(vmem_limit_bytes=16 << 20),
        cost_estimate=pl.CostEstimate(flops=0, bytes_accessed=2 * blocks.size * blocks.dtype.itemsize, transcendentals=0),
        name="place",
    )(blocks)


def pair_weights(images, texts, targets, columns, scale, shift):
    scores = scale * lax.dot_general(
        images, texts, (((1,), (1,)), ((), ())), preferred_element_type=jnp.float32
    ) + shift
    grid = jnp.where(
        targets[:, None] == columns[None, :],
        -scale * jax.nn.sigmoid(-scores),
        scale * jax.nn.sigmoid(scores),
    )
    return grid.astype(jnp.bfloat16)


def across(grid, other):
    return lax.dot_general(grid, other, (((0,), (0,)), ((), ())), preferred_element_type=jnp.float32)


def body(
    visual_fragments,
    widening_kernel,
    narrowing_kernel,
    caption_outputs,
    earlier_averaged,
    match_targets,
    score_scaling,
    score_shift,
):
    stages = lax.axis_size("pipe")
    depth = lax.axis_size("z")
    stage_id = lax.axis_index("pipe")
    z_id = lax.axis_index("z")
    around = lax.axis_size("yh") * lax.axis_size("core")
    around_id = lax.axis_index("yh") * lax.axis_size("core") + lax.axis_index("core")
    micros, img_mb, patch_count, width = visual_fragments.shape
    tok_rows = img_mb * patch_count
    plane = stages * around
    scale = score_scaling[0]
    shift = score_shift[0]
    texts_dev = caption_outputs.shape[0]
    prior_dev = earlier_averaged.shape[0]

    up = widening_kernel[0].T
    down = narrowing_kernel[0]
    both = jnp.stack([up, down])
    both = jnp.concatenate([both, swap(both, "yh")], axis=1)
    units = both.shape[1]
    padded = -(-units // 8) * 8
    both = jnp.pad(both, ((0, 0), (0, padded - units), (0, 0)))
    depth_blocks = lax.all_gather(both.reshape(2 * padded, width), "z", axis=0, tiled=True)

    text_own = unit_rows(caption_outputs)
    prior_own = unit_rows(earlier_averaged)
    lanes = texts_dev * width // 128
    texts = lax.all_gather(text_own, "z", axis=0, tiled=False).reshape(depth * texts_dev, width)
    priors = share_rows(prior_own, PLANE, plane).reshape(plane * prior_dev, width)
    labels = lax.dynamic_index_in_dim(
        match_targets.reshape(stages, depth, around, img_mb + prior_dev), z_id, 1, keepdims=False
    )
    columns = (
        ((stage_id * depth + jnp.arange(depth, dtype=jnp.int32)) * around + around_id) * texts_dev
    )[:, None] + jnp.arange(texts_dev, dtype=jnp.int32)[None, :]
    columns = columns.reshape(-1)
    grid = pair_weights(priors, texts, labels[:, :, img_mb:].reshape(-1), columns, scale, shift)
    prior_part = jnp.dot(grid, texts, preferred_element_type=jnp.float32).astype(jnp.bfloat16)
    prior_part = lax.all_to_all(prior_part.reshape(plane, prior_dev, width), PLANE, 0, 0)
    prior_grad = jnp.sum(prior_part.astype(jnp.float32), axis=0)
    text_early = across(grid, priors)
    first = (stage_id == 0).astype(jnp.int32).reshape(1)
    depth_blocks, prior_grad, text_early, first = lax.optimization_barrier((depth_blocks, prior_grad, text_early, first))
    other_blocks = swap(depth_blocks, "core")
    weights = tuple(half.reshape(depth, 2, padded, width) for half in (place(depth_blocks), other_blocks))

    groups = micros // GROUP
    panels = visual_fragments.reshape(groups, GROUP * tok_rows, width)
    last = STAGE_GAP * (stages - 1)
    sent = []
    pooled = []
    for slot in range(groups + last):
        pick = min(slot, groups - 1)
        if slot < STAGE_GAP:
            take, carried = "panel", panels[pick]
        else:
            take, carried = ("either" if slot < groups else "carried"), sent[slot - STAGE_GAP]
        done = slot >= last
        results = stage(first, panels, pick, carried, weights, GROUP * img_mb if done else 0, take)
        moved = results[0]
        if done:
            pooled.append(results[1])
        hops = [(at, at + 1) for at in range(stages - 1) if 0 <= slot - STAGE_GAP * at < groups]
        sent.append(lax.ppermute(moved, "pipe", hops) if hops else None)
    tower_own = unit_rows(jnp.concatenate(pooled, axis=0))

    tower = share_rows(tower_own, PLANE, plane).reshape(stages, around, micros, width)[stages - 1]
    tower = tower.reshape(around * micros, width)
    tower_labels = labels[:, :, 0].T.reshape(-1)
    tower_grid = pair_weights(tower, texts, tower_labels, columns, scale, shift)
    text_part = text_early + across(tower_grid, tower)
    text_part = text_part.astype(jnp.bfloat16).reshape(depth, lanes, 128)
    text_part = lax.all_to_all(text_part, "z", 0, 0)
    tower_part = jnp.dot(tower_grid, texts, preferred_element_type=jnp.float32).astype(jnp.bfloat16)
    tower_part = tower_part.reshape(around, micros, width).transpose(1, 0, 2)
    tower_part = tower_part.reshape(plane, img_mb * width // 128, 128)
    text_part, tower_part = lax.optimization_barrier((text_part, tower_part))
    text_grad = jnp.sum(text_part.astype(jnp.float32), axis=0).reshape(texts_dev, width)
    tower_part = lax.all_to_all(tower_part, PLANE, 0, 0)
    tower_grad = jnp.sum(tower_part.astype(jnp.float32), axis=0).reshape(img_mb, width)
    return jnp.concatenate([tower_grad, prior_grad], axis=0), text_grad


def solution(mesh):
    sizes = dict(mesh.shape)
    stages = sizes["pipe"]
    fine = Mesh(mesh.devices.reshape(stages, sizes["dp"] // 4, 2, 2), EVERY)
    data = ("z", "yh", "core")
    placed = (
        P(None, data, None, None),
        P("pipe", None, data),
        P("pipe", data, None),
        P(EVERY, None),
        P(EVERY, None),
        P(),
        P(),
        P(),
    )
    return jax.shard_map(
        body,
        mesh=fine,
        in_specs=placed,
        out_specs=(P(EVERY, None), P(EVERY, None)),
        check_vma=False,
    )
```

```python
import functools

import jax
import jax.numpy as jnp
from jax import lax
from jax.experimental import pallas as pl
from jax.experimental.pallas import tpu as pltpu
from jax.sharding import Mesh, PartitionSpec as P

STAGE_GAP = 2
GROUP = 1
PLANE = ("pipe", "yh", "core")
EVERY = ("pipe", "z", "yh", "core")


def unit_rows(values):
    values = values.astype(jnp.float32)
    total = jnp.sum(values * values, axis=-1, keepdims=True)
    return (values * lax.rsqrt(total + 1e-06)).astype(jnp.bfloat16)


def share_rows(rows, axes, count):
    copies = jnp.broadcast_to(rows[None], (count,) + rows.shape)
    return lax.all_to_all(copies, axes, 0, 0)


def swap(value, axis):
    return lax.ppermute(value, axis, [(0, 1), (1, 0)])


def stage_kernel(*refs, take, slot, images):
    refs = list(refs)
    if take != "carried":
        place_ref = refs.pop(0)
    panels_ref = refs.pop(0) if take != "carried" else None
    carried_ref = refs.pop(0) if take != "panel" else None
    own_ref, other_ref, out_ref = refs[:3]
    pooled_ref = refs[3] if images else None
    (act_ref,) = refs[-1:]
    rows, width = out_ref.shape
    if take == "carried":
        hidden = carried_ref[...]
    else:
        hidden = panels_ref[jnp.clip(slot - place_ref[1], 0, panels_ref.shape[0] - 1)]
        if take == "either":
            hidden = jnp.where(place_ref[0] == 1, hidden, carried_ref[...])
    values = hidden.astype(jnp.float32)
    centre = jnp.mean(values, axis=-1, keepdims=True)
    shifted = values - centre
    variance = jnp.mean(shifted * shifted, axis=-1, keepdims=True)
    normed = (shifted * lax.rsqrt(variance + 1e-06)).astype(jnp.bfloat16)
    blocks, _, block, _ = own_ref.shape
    units = blocks * block
    total = values
    for half, ref in enumerate((own_ref, other_ref)):
        pre_act = lax.dot_general(
            normed,
            ref[:, 0].reshape(units, width),
            (((1,), (1,)), ((), ())),
            preferred_element_type=jnp.float32,
        )
        act_ref[:, half * units : (half + 1) * units] = jax.nn.gelu(pre_act, approximate=True).astype(jnp.bfloat16)
    for half, ref in enumerate((own_ref, other_ref)):
        total += jnp.dot(
            act_ref[:, half * units : (half + 1) * units],
            ref[:, 1].reshape(units, width),
            preferred_element_type=jnp.float32,
        )
    updated = total.astype(jnp.bfloat16)
    out_ref[...] = updated
    for image in range(images):
        patches = rows // images
        mean = jnp.mean(updated[image * patches : (image + 1) * patches].astype(jnp.float32), axis=0, keepdims=True)
        pooled_ref[image : image + 1] = mean


def stage(spot, panels, slot, carried, weights, images, take):
    rows, width = panels.shape[1:]
    units = weights[0].shape[0] * weights[0].shape[2]
    whole = pl.BlockSpec(memory_space=pltpu.VMEM)
    operands = {"panel": (panels,), "carried": (carried,), "either": (panels, carried)}[take] + tuple(weights)
    specs = [whole] * len(operands)
    if take != "carried":
        operands = (spot,) + operands
        specs = [pl.BlockSpec(memory_space=pltpu.SMEM)] + specs
    shapes = [jax.ShapeDtypeStruct((rows, width), jnp.bfloat16)]
    if images:
        shapes.append(jax.ShapeDtypeStruct((images, width), jnp.float32))
    return pl.pallas_call(
        functools.partial(stage_kernel, take=take, slot=slot, images=images),
        in_specs=specs,
        out_specs=[whole] * len(shapes),
        out_shape=shapes,
        scratch_shapes=[
            pltpu.VMEM((rows, 2 * units), jnp.bfloat16),
        ],
        compiler_params=pltpu.CompilerParams(vmem_limit_bytes=24 << 20),
        cost_estimate=pl.CostEstimate(
            flops=8 * rows * width * units,
            bytes_accessed=8 * width * units,
            transcendentals=2 * rows * units,
        ),
        name="stage",
    )(*operands)


def place_kernel(blocks_ref, placed_ref, sem):
    copy = pltpu.make_async_copy(blocks_ref, placed_ref, sem)
    copy.start()
    copy.wait()


def place(blocks):
    return pl.pallas_call(
        place_kernel,
        in_specs=[pl.BlockSpec(memory_space=pltpu.VMEM)],
        out_specs=pl.BlockSpec(memory_space=pltpu.VMEM),
        out_shape=jax.ShapeDtypeStruct(blocks.shape, blocks.dtype),
        scratch_shapes=[pltpu.SemaphoreType.DMA],
        compiler_params=pltpu.CompilerParams(vmem_limit_bytes=16 << 20),
        cost_estimate=pl.CostEstimate(flops=0, bytes_accessed=2 * blocks.size * blocks.dtype.itemsize, transcendentals=0),
        name="place",
    )(blocks)


def pair_weights(images, texts, targets, columns, scale, shift):
    scores = scale * lax.dot_general(
        images, texts, (((1,), (1,)), ((), ())), preferred_element_type=jnp.float32
    ) + shift
    grid = jnp.where(
        targets[:, None] == columns[None, :],
        -scale * jax.nn.sigmoid(-scores),
        scale * jax.nn.sigmoid(scores),
    )
    return grid.astype(jnp.bfloat16)


def across(grid, other):
    return lax.dot_general(grid, other, (((0,), (0,)), ((), ())), preferred_element_type=jnp.float32)


def body(
    visual_fragments,
    widening_kernel,
    narrowing_kernel,
    caption_outputs,
    earlier_averaged,
    match_targets,
    score_scaling,
    score_shift,
):
    stages = lax.axis_size("pipe")
    depth = lax.axis_size("z")
    stage_id = lax.axis_index("pipe")
    z_id = lax.axis_index("z")
    around = lax.axis_size("yh") * lax.axis_size("core")
    around_id = lax.axis_index("yh") * lax.axis_size("core") + lax.axis_index("core")
    micros, img_mb, patch_count, width = visual_fragments.shape
    tok_rows = img_mb * patch_count
    plane = stages * around
    scale = score_scaling[0]
    shift = score_shift[0]
    texts_dev = caption_outputs.shape[0]
    prior_dev = earlier_averaged.shape[0]

    up = widening_kernel[0].T
    down = narrowing_kernel[0]
    both = jnp.stack([up, down])
    both = jnp.concatenate([both, swap(both, "yh")], axis=1)
    units = both.shape[1]
    padded = -(-units // 8) * 8
    both = jnp.pad(both, ((0, 0), (0, padded - units), (0, 0)))
    depth_blocks = lax.all_gather(both.reshape(2 * padded, width), "z", axis=0, tiled=True)

    text_own = unit_rows(caption_outputs)
    prior_own = unit_rows(earlier_averaged)
    lanes = texts_dev * width // 128
    texts = lax.all_gather(text_own, "z", axis=0, tiled=False).reshape(depth * texts_dev, width)
    priors = share_rows(prior_own, PLANE, plane).reshape(plane * prior_dev, width)
    labels = lax.dynamic_index_in_dim(
        match_targets.reshape(stages, depth, around, img_mb + prior_dev), z_id, 1, keepdims=False
    )
    columns = (
        ((stage_id * depth + jnp.arange(depth, dtype=jnp.int32)) * around + around_id) * texts_dev
    )[:, None] + jnp.arange(texts_dev, dtype=jnp.int32)[None, :]
    columns = columns.reshape(-1)
    grid = pair_weights(priors, texts, labels[:, :, img_mb:].reshape(-1), columns, scale, shift)
    prior_part = jnp.dot(grid, texts, preferred_element_type=jnp.float32).astype(jnp.bfloat16)
    prior_part = lax.all_to_all(prior_part.reshape(plane, prior_dev, width), PLANE, 0, 0)
    prior_grad = jnp.sum(prior_part.astype(jnp.float32), axis=0)
    text_early = across(grid, priors)
    core_id = lax.axis_index("core")
    spot = jnp.stack([(stage_id == 0).astype(jnp.int32), core_id])
    begin = (core_id * GROUP * img_mb).astype(jnp.uint32)
    depth_blocks, prior_grad, text_early, spot, begin = lax.optimization_barrier(
        (depth_blocks, prior_grad, text_early, spot, begin)
    )
    other_blocks = swap(depth_blocks, "core")
    weights = tuple(half.reshape(depth, 2, padded, width) for half in (place(depth_blocks), other_blocks))

    cores = lax.axis_size("core")
    groups = micros // GROUP
    panels = visual_fragments.reshape(groups, GROUP * tok_rows, width)
    last = STAGE_GAP * (stages - 1)
    sent = []
    pooled = []
    for slot in range(groups + last + cores - 1):
        carried = sent[slot - STAGE_GAP] if slot >= STAGE_GAP else None
        take = "panel" if slot < STAGE_GAP else "either" if slot < groups + cores - 1 else "carried"
        done = slot >= last
        results = stage(spot, panels, slot, carried, weights, GROUP * img_mb if done else 0, take)
        moved = results[0]
        if done:
            pooled.append(results[1])
        hops = [
            (at * cores + core, (at + 1) * cores + core)
            for at in range(stages - 1)
            for core in range(cores)
            if 0 <= slot - core - STAGE_GAP * at < groups
        ]
        sent.append(lax.ppermute(moved, ("pipe", "core"), hops) if hops else None)
    pooled = lax.dynamic_slice(
        jnp.concatenate(pooled, axis=0), (begin, jnp.zeros((), jnp.uint32)), (micros * img_mb, width)
    )
    tower_own = unit_rows(pooled)

    tower = share_rows(tower_own, PLANE, plane).reshape(stages, around, micros, width)[stages - 1]
    tower = tower.reshape(around * micros, width)
    tower_labels = labels[:, :, 0].T.reshape(-1)
    tower_grid = pair_weights(tower, texts, tower_labels, columns, scale, shift)
    text_part = text_early + across(tower_grid, tower)
    text_part = text_part.astype(jnp.bfloat16).reshape(depth, lanes, 128)
    text_part = lax.all_to_all(text_part, "z", 0, 0)
    tower_part = jnp.dot(tower_grid, texts, preferred_element_type=jnp.float32).astype(jnp.bfloat16)
    tower_part = tower_part.reshape(around, micros, width).transpose(1, 0, 2)
    tower_part = tower_part.reshape(plane, img_mb * width // 128, 128)
    text_part, tower_part = lax.optimization_barrier((text_part, tower_part))
    text_grad = jnp.sum(text_part.astype(jnp.float32), axis=0).reshape(texts_dev, width)
    tower_part = lax.all_to_all(tower_part, PLANE, 0, 0)
    tower_grad = jnp.sum(tower_part.astype(jnp.float32), axis=0).reshape(img_mb, width)
    return jnp.concatenate([tower_grad, prior_grad], axis=0), text_grad


def solution(mesh):
    sizes = dict(mesh.shape)
    stages = sizes["pipe"]
    fine = Mesh(mesh.devices.reshape(stages, sizes["dp"] // 4, 2, 2), EVERY)
    data = ("z", "yh", "core")
    placed = (
        P(None, data, None, None),
        P("pipe", None, data),
        P("pipe", data, None),
        P(EVERY, None),
        P(EVERY, None),
        P(),
        P(),
        P(),
    )
    return jax.shard_map(
        body,
        mesh=fine,
        in_specs=placed,
        out_specs=(P(EVERY, None), P(EVERY, None)),
        check_vma=False,
    )
```
